128 devices in a mesh: row: 64 (over z, y, x), col: 2 (over core).
Axes of the slice: x: 4, y: 4, z: 4, core: 2. Of those that a mesh axis runs over, the one named last changes fastest.
Arguments:
- factor: bfloat16 [2, 8192, 65536], P(None, 'row', 'col'), may hold values from -40 to 40
- scales: float32 [2, 64, 512], P(None, 'row', 'col'), may hold values from 0 to 1, as said below
- coords: float32 [2, 2, 8192], replicated, may hold values from 0 to 1
- jitter: float32 [1], replicated, may hold values from 1 to 2
Outputs:
- new_columns: float32 [2, 8192, 256], P(None, ('row', 'col'))
The draws below stay inside these ranges and needn't reach their ends.
Inputs may be any that keep to these rules, and one draw needn't show every extreme that they name: `scales`: positive.
All inputs are finite; a program needn't handle non-finite values.
Results may differ from the reference program's by a relative error of at most 0.0003.
Values may be sent and summed in bfloat16 or wider, within the bound.
No kernel may reach another device: no remote copies, remote signals or barrier semaphores. Data moves between devices by JAX's collectives and lax.ppermute only.
A program may use at most 192 MiB of HBM per device.

```python
import math
import jax
import jax.numpy as jnp
from jax import lax

PANEL = 128
CYC = 2
KF = 65536
KB = 512
N_ROW = 64


def draw_factor(key, part):
    key_lead = jax.random.fold_in(key, 11)
    key_mix = jax.random.fold_in(key, 12)
    leading = jnp.clip(jax.random.normal(key_lead, (2 * PANEL, KF), jnp.float32), -4.0, 4.0)

    def one_block(index):
        block_key = jax.random.fold_in(key_mix, index)
        key_one, key_two = jax.random.split(block_key, 2)
        mixing = 0.5 * jax.random.normal(key_one, (PANEL, 2 * PANEL), jnp.float32)
        noise = jax.random.normal(key_two, (PANEL, KF), jnp.float32)
        mixed = jnp.clip(jnp.dot(mixing, leading) + noise, -40.0, 40.0)
        own_rows = lax.dynamic_slice_in_dim(leading, jnp.minimum(index, 1) * PANEL, PANEL, 0)
        return jnp.where(index < 2, own_rows, mixed).astype(jnp.bfloat16)
    stacked = lax.map(one_block, jnp.arange(CYC * N_ROW, dtype=jnp.int32))
    return stacked.reshape(CYC, N_ROW * PANEL, KF)


def draw_scales(key, part):
    level = jax.random.uniform(jax.random.fold_in(key, 21), (CYC, N_ROW, KB), jnp.float32, math.log(0.3), math.log(3.0))
    return jnp.exp(level) * (0.25 / math.sqrt(KF))


def setup_inputs(seed: int = 0) -> dict:
    seeds = jax.random.split(jax.random.key(seed), 5)
    return {
        "factor": draw_factor(jax.random.fold_in(seeds[4], 71), 0),
        "scales": draw_scales(jax.random.fold_in(seeds[4], 71), 0),
        "coords": jnp.clip(jax.random.uniform(seeds[2], (2, CYC, N_ROW * PANEL), jnp.float32, 0.0, 1.0), 0.0, 1.0),
        "jitter": jnp.clip(jax.random.uniform(seeds[3], (1,), jnp.float32, 1.0, 2.0), 1.0, 2.0),
    }


SQRT_THREE = 1.7320508075688772
LENGTH_SCALE = 0.25

def matern(left_pts, right_pts):
    diff_x = left_pts[0][:, None] - right_pts[0][None, :]
    diff_y = left_pts[1][:, None] - right_pts[1][None, :]
    scaled = SQRT_THREE * jnp.sqrt(diff_x * diff_x + diff_y * diff_y) / LENGTH_SCALE
    return (1.0 + scaled) * jnp.exp(-scaled)

def dequantize(block, scale_row):
    widened = block.astype(jnp.float32).reshape(PANEL, KB, PANEL) * scale_row[None, :, None]
    return widened.reshape(PANEL, KF).astype(jnp.bfloat16)

def reference(factor, scales, coords, jitter):
    lead_width = 2 * PANEL
    block_count = CYC * N_ROW
    blocks = factor.reshape(block_count, PANEL, KF)
    block_scales = scales.reshape(block_count, KB)
    leading = jnp.concatenate([dequantize(blocks[0], block_scales[0]), dequantize(blocks[1], block_scales[1])], axis=0)

    def one_block(inputs):
        return lax.dot_general(dequantize(inputs[0], inputs[1]).astype(jnp.float32), leading.astype(jnp.float32), (((1,), (1,)), ((), ())), preferred_element_type=jnp.float32)
    products = lax.map(one_block, (blocks, block_scales)).reshape(block_count * PANEL, lead_width)
    points = coords.reshape(2, block_count * PANEL)
    lead_pts = points[:, :lead_width]
    rows_all = jnp.arange(block_count * PANEL, dtype=jnp.int32)
    identity_mask = (rows_all[:, None] == jnp.arange(lead_width, dtype=jnp.int32)[None, :]).astype(jnp.float32)
    window = matern(points, lead_pts) + jitter[0] * identity_mask - products
    factor_low = jnp.linalg.cholesky(window[:lead_width])
    result = jax.scipy.linalg.solve_triangular(factor_low, window.T, lower=True).T
    return result.reshape(CYC, N_ROW * PANEL, lead_width)
```

```python
import jax
import jax.numpy as jnp
from jax import lax
from jax.experimental import pallas as pl
from jax.experimental.pallas import tpu as pltpu
from jax.sharding import PartitionSpec as P

PANEL = 128
LEAD = 2 * PANEL
SQRT_THREE = 1.7320508075688772
LENGTH_SCALE = 0.25
HIGHEST = lax.Precision.HIGHEST
TN = (((1,), (1,)), ((), ()))
TT = (((0,), (0,)), ((), ()))

STEP = 2048
SUB = 32


def vmem():
    return pl.BlockSpec(memory_space=pltpu.VMEM)


def smem():
    return pl.BlockSpec(memory_space=pltpu.SMEM)


def scaled(block, scale_ref, row, first):
    parts = [
        (block[:, j * PANEL : (j + 1) * PANEL].astype(jnp.float32) * scale_ref[row, first + j]).astype(jnp.bfloat16)
        for j in range(block.shape[1] // PANEL)
    ]
    return jnp.concatenate(parts, axis=1)


def dequant_kernel(scale_ref, factor_ref, out_ref):
    first = pl.program_id(0) * (STEP // PANEL)
    out_ref[...] = scaled(factor_ref[0], scale_ref, 0, first)


def dequantize_lead(factor, scales):
    width = factor.shape[2]
    return pl.pallas_call(
        dequant_kernel,
        grid=(width // STEP,),
        in_specs=[smem(), pl.BlockSpec((1, PANEL, STEP), lambda k: (0, 0, k))],
        out_specs=pl.BlockSpec((PANEL, STEP), lambda k: (0, k)),
        out_shape=jax.ShapeDtypeStruct((PANEL, width), jnp.bfloat16),
        name="dequantize_lead",
    )(scales, factor)


def products_kernel(col_ref, scale_ref, factor_ref, one_ref, two_ref, send_ref, keep_ref, acc_ref):
    step = pl.program_id(0)

    @pl.when(step == 0)
    def _():
        acc_ref[...] = jnp.zeros_like(acc_ref)

    first = step * (STEP // PANEL)
    lead = jnp.concatenate([one_ref[...], two_ref[...]], axis=0)
    left = jnp.concatenate(
        [scaled(factor_ref[0], scale_ref, 0, first), scaled(factor_ref[1], scale_ref, 1, first), lead], axis=0
    )
    acc_ref[...] += lax.dot_general(left, lead, TN, preferred_element_type=jnp.float32)

    @pl.when(step == pl.num_programs(0) - 1)
    def _():
        share = PANEL // 2
        mine = col_ref[0] * share
        other = share - mine
        for c in range(2):
            here = pl.ds(c * share, share)
            keep_ref[here, :] = acc_ref[pl.ds(pl.multiple_of(c * PANEL + mine, share), share), :]
            send_ref[here, :] = acc_ref[pl.ds(pl.multiple_of(c * PANEL + other, share), share), :]
        keep_ref[PANEL:, :] = acc_ref[LEAD:, :]
        send_ref[PANEL:, :] = acc_ref[LEAD:, :]


def partial_products(col_index, factor, scales, one, two):
    width = factor.shape[2]
    out = jax.ShapeDtypeStruct((PANEL + LEAD, LEAD), jnp.float32)
    return pl.pallas_call(
        products_kernel,
        grid=(width // STEP,),
        in_specs=[
            smem(),
            smem(),
            pl.BlockSpec((2, PANEL, STEP), lambda k: (0, 0, k)),
            pl.BlockSpec((PANEL, STEP), lambda k: (0, k)),
            pl.BlockSpec((PANEL, STEP), lambda k: (0, k)),
        ],
        out_specs=[pl.BlockSpec((PANEL + LEAD, LEAD), lambda k: (0, 0))] * 2,
        out_shape=[out, out],
        scratch_shapes=[pltpu.VMEM((2 * LEAD, LEAD), jnp.float32)],
        name="partial_products",
    )(col_index, scales, factor, one, two)


def matern(left, right_x, right_y):
    diff_x = left[:, 0:1] - right_x
    diff_y = left[:, 1:2] - right_y
    t = SQRT_THREE * jnp.sqrt(diff_x * diff_x + diff_y * diff_y) / LENGTH_SCALE
    return (1.0 + t) * jnp.exp(-t)


def finish_kernel(first_ref, jitter_ref, keep_ref, recv_ref, own_ref, leadc_ref, leadr_ref, out_ref, work_ref):
    jitter = jitter_ref[0]
    lead_x, lead_y = leadr_ref[0:1, :], leadr_ref[1:2, :]
    share = PANEL // 2

    def eye(rows, first):
        row = lax.broadcasted_iota(jnp.int32, (rows, LEAD), 0) + first
        col = lax.broadcasted_iota(jnp.int32, (rows, LEAD), 1)
        return jnp.where(row == col, jitter, 0.0)

    block = matern(leadc_ref[...], lead_x, lead_y) + eye(LEAD, 0) - (keep_ref[PANEL:, :] + recv_ref[PANEL:, :])
    work_ref[:, :LEAD] = 0.5 * (block + block.T)
    diag = jnp.concatenate([eye(share, first_ref[0]), eye(share, first_ref[1])], axis=0)
    own = matern(own_ref[...], lead_x, lead_y) + diag - (keep_ref[:PANEL, :] + recv_ref[:PANEL, :])
    work_ref[:, LEAD:] = own.T

    rows = lax.broadcasted_iota(jnp.int32, (SUB, 1), 0)
    for top in range(0, LEAD, SUB):
        start = top // PANEL * PANEL
        part = work_ref[top : top + SUB, start:]
        for k in range(SUB):
            at = top + k - start
            column = part[:, at : at + 1]
            inv = lax.rsqrt(part[k : k + 1, at : at + 1])
            pivot = part[k : k + 1, :] * inv
            part = jnp.where(rows > k, part - (column * inv) * pivot, jnp.where(rows == k, pivot, part))
        work_ref[top : top + SUB, start:] = part
        low = top + SUB
        if low < LEAD:
            begin = low // PANEL * PANEL
            change = lax.dot_general(
                part[:, begin - start : LEAD - start], part[:, begin - start :], TT,
                precision=HIGHEST, preferred_element_type=jnp.float32,
            )
            work_ref[low:, begin:] -= change[low - begin :, :]
    out_ref[...] = work_ref[:, LEAD:].T


def finish(first, jitter, keep, recv, own, leadc, leadr):
    return pl.pallas_call(
        finish_kernel,
        in_specs=[smem(), smem(), vmem(), vmem(), vmem(), vmem(), vmem()],
        out_specs=vmem(),
        out_shape=jax.ShapeDtypeStruct((PANEL, LEAD), jnp.float32),
        scratch_shapes=[pltpu.VMEM((LEAD, LEAD + PANEL), jnp.float32)],
        name="finish",
    )(first, jitter, keep, recv, own, leadc, leadr)


def tail(factor, scales, coords, jitter, one, two):
    row_index = lax.axis_index("row")
    col_index = lax.axis_index("col")
    share = PANEL // 2
    begin = row_index * PANEL + col_index * share
    own = lax.dynamic_slice_in_dim(coords, begin, share, 2).reshape(2, PANEL)
    lead = coords[:, 0, :LEAD]
    first = jnp.stack([begin, begin + coords.shape[2]]).astype(jnp.int32)
    send, keep = partial_products(col_index[None].astype(jnp.int32), factor, scales[:, 0], one, two)
    recv = lax.ppermute(send, "col", [(0, 1), (1, 0)])
    out = finish(first, jitter, keep, recv, own.T, lead.T, lead)
    return out.reshape(2, share, LEAD)


def on_device(factor, scales, coords, jitter):
    row_index = lax.axis_index("row")
    own = dequantize_lead(factor, scales[:, 0])
    zero = jnp.zeros_like(own)
    one, two = lax.psum((jnp.where(row_index == 0, own, zero), jnp.where(row_index == 1, own, zero)), "row")
    return tail(factor, scales, coords, jitter, one, two)


def solution(mesh):
    placed = (P(None, "row", "col"), P(None, "row", "col"), P(), P())
    return jax.shard_map(
        on_device,
        mesh=mesh,
        in_specs=placed,
        out_specs=P(None, ("row", "col"), None),
        check_vma=False,
    )
```

```python
import functools

import jax
import jax.numpy as jnp
from jax import lax
from jax.experimental import pallas as pl
from jax.experimental.pallas import tpu as pltpu
from jax.sharding import PartitionSpec as P

PANEL = 128
LEAD = 2 * PANEL
SQRT_THREE = 1.7320508075688772
LENGTH_SCALE = 0.25
HIGHEST = lax.Precision.HIGHEST
TN = (((1,), (1,)), ((), ()))
TT = (((0,), (0,)), ((), ()))

SUB = 32
MINI = 4
QUARTER = PANEL // 4
SIDE = 4
CHIPS = SIDE**3
ORDERS = ((("y", "z", "x"), ("z", "x", "y")), (("x", "y", "z"), ("x", "y", "z")))
BLOCKS = (176, 80)
SLOTS = (1, 2)
PARTS = range(2)
PIECES = 4


def vmem():
    return pl.BlockSpec(memory_space=pltpu.VMEM)


def smem():
    return pl.BlockSpec(memory_space=pltpu.SMEM)


def anywhere():
    return pl.BlockSpec(memory_space=pltpu.HBM)


def width(part):
    return BLOCKS[part] // SIDE * PANEL


def coordinates(chip):
    return {"x": chip % SIDE, "y": chip // SIDE % SIDE, "z": chip // (SIDE * SIDE)}


def number(place):
    return place["x"] + SIDE * place["y"] + SIDE * SIDE * place["z"]


def here(part, axis, root=0):
    place = coordinates(lax.axis_index("row"))
    first, second = [place[order[axis]] - (root if order[axis] == "x" else 0) for order in ORDERS[part]]
    distance = first if ORDERS[part][0] == ORDERS[part][1] else jnp.where(lax.axis_index("col") == 0, first, second)
    return lax.rem(distance + SIDE, SIDE)


def first_block(part, behind):
    return sum(BLOCKS[:part]) + lax.rem(here(part, 0) + SIDE - behind, SIDE) * (BLOCKS[part] // SIDE)


def quarter(part, behind):
    q = lax.rem(here(part, 1) + SIDE - behind, SIDE)
    return pl.ds(pl.multiple_of(q * QUARTER, QUARTER), QUARTER)


def scale_in_place(ref, begin, count, scale_ref, row, first):
    for j in range(count):
        columns = slice((begin + j) * PANEL, (begin + j + 1) * PANEL)
        ref[:, columns] = (ref[:, columns].astype(jnp.float32) * scale_ref[row, 0, first + begin + j]).astype(jnp.bfloat16)


def dequant_kernel(part, cycle, scale_ref, factor_ref, *refs):
    outs, work_ref, in_sems, out_sems = refs[:SIDE], refs[SIDE], refs[SIDE + 1], refs[SIDE + 2]
    columns = work_ref.shape[2]

    def fetch(s):
        begin = pl.multiple_of(first_block(part, SIDE - s) * PANEL, PANEL)
        return pltpu.make_async_copy(factor_ref.at[cycle, :, pl.ds(begin, columns)], work_ref.at[s], in_sems.at[s])

    def put(s):
        return pltpu.make_async_copy(work_ref.at[s], outs[s], out_sems.at[s])

    for s in range(SIDE):
        fetch(s).start()
    for s in range(SIDE):
        fetch(s).wait()
        scale_in_place(work_ref.at[s], 0, columns // PANEL, scale_ref, cycle, first_block(part, SIDE - s))
        put(s).start()
    for s in range(SIDE):
        put(s).wait()


def dequantize_chunks(part, cycle, factor, scales):
    shape = (PANEL, width(part))
    return pl.pallas_call(
        functools.partial(dequant_kernel, part, cycle),
        in_specs=[smem(), anywhere()],
        out_specs=[anywhere()] * SIDE,
        out_shape=[jax.ShapeDtypeStruct(shape, jnp.bfloat16)] * SIDE,
        scratch_shapes=[
            pltpu.VMEM((SIDE, *shape), jnp.bfloat16),
            pltpu.SemaphoreType.DMA((SIDE,)),
            pltpu.SemaphoreType.DMA((SIDE,)),
        ],
        name="dequantize_chunks",
    )(scales, factor)


def gather_copies(moves, sems):
    for n, (wanted, sources, target) in enumerate(moves):
        if len(sources) == 1:
            pltpu.make_async_copy(sources[0], target, sems.at[n]).start()
            continue
        for s, source in enumerate(sources):

            @pl.when(wanted == s)
            def _():
                pltpu.make_async_copy(source, target, sems.at[n]).start()

    for n, (_, sources, target) in enumerate(moves):
        pltpu.make_async_copy(sources[0], target, sems.at[n]).wait()


def of_part(refs, part):
    return refs[part * SIDE : (part + 1) * SIDE]


def pick_rows_kernel(*refs):
    ins, outs, sems = refs[: 2 * SIDE], refs[2 * SIDE : -1], refs[-1]
    moves = []
    for part in PARTS:
        for t in range(SIDE):
            for r in range(SLOTS[part]):
                sources = [ref.at[quarter(part, SIDE - t), :] for ref in of_part(ins, part)]
                moves.append((here(part, 0, r), sources, of_part(outs, part)[t].at[r]))
    gather_copies(moves, sems)


def pick_rows(state):
    out = pl.pallas_call(
        pick_rows_kernel,
        in_specs=[anywhere()] * (2 * SIDE),
        out_specs=[vmem()] * (2 * SIDE),
        out_shape=[
            jax.ShapeDtypeStruct((SLOTS[part], QUARTER, width(part)), jnp.bfloat16)
            for part in PARTS
            for _ in range(SIDE)
        ],
        scratch_shapes=[pltpu.SemaphoreType.DMA((SIDE * sum(SLOTS),))],
        name="pick_rows",
    )(*sum(state, []))
    return [out[:SIDE], out[SIDE:]]


def pick_pieces_kernel(*refs):
    ins, outs, sems = refs[: 2 * SIDE], (refs[2 * SIDE], refs[2 * SIDE + 1], refs[2 * SIDE + 2]), refs[-1]
    targets = [[outs[0].at[0], outs[1].at[0]], [outs[2].at[0], outs[2].at[1]]]
    moves = []
    for part in PARTS:
        for r in range(2):
            sources = [ref.at[min(r, SLOTS[part] - 1)] for ref in of_part(ins, part)]
            moves.append((here(part, 1, r), sources, targets[part][r]))
    gather_copies(moves, sems)


def pick_pieces(state):
    return pl.pallas_call(
        pick_pieces_kernel,
        in_specs=[anywhere()] * (2 * SIDE),
        out_specs=[vmem()] * 3,
        out_shape=[
            jax.ShapeDtypeStruct((slots, QUARTER, width(part)), jnp.bfloat16) for part, slots in ((0, 1), (0, 1), (1, 2))
        ],
        scratch_shapes=[pltpu.SemaphoreType.DMA((4,))],
        name="pick_pieces",
    )(*sum(state, []))


def pick_shared_kernel(*refs):
    zero, one, both, outs, sems = refs[:4], refs[4:8], refs[8:12], refs[12:14], refs[-1]
    second = lax.axis_index("col") == 1
    moves = [(here(0, 2, 0), [ref.at[0] for ref in zero], outs[0].at[0])]
    wanted = here(0, 2, 1) + jnp.where(second, SIDE, 0)
    moves.append((wanted, [ref.at[0] for ref in zero] + [ref.at[0] for ref in one], outs[0].at[1]))
    moves += [(here(1, 2, r), [ref.at[r] for ref in both], outs[1].at[r]) for r in range(2)]
    gather_copies(moves, sems)


def pick_shared(zero, one, both):
    return pl.pallas_call(
        pick_shared_kernel,
        in_specs=[anywhere()] * (3 * SIDE),
        out_specs=[vmem()] * 2,
        out_shape=[jax.ShapeDtypeStruct((2, QUARTER, width(part)), jnp.bfloat16) for part in PARTS],
        scratch_shapes=[pltpu.SemaphoreType.DMA((4,))],
        name="pick_shared",
    )(*zero, *one, *both)


def assemble_kernel(*refs):
    ins, outs, sems = refs[: 2 * SIDE], refs[2 * SIDE : -1], refs[-1]
    moves = []
    for part in PARTS:
        for t in range(SIDE):
            for r in range(2):
                moves.append((0, [of_part(ins, part)[t].at[r]], outs[2 * part + r].at[quarter(part, t), :]))
    gather_copies(moves, sems)


def assemble(state):
    return pl.pallas_call(
        assemble_kernel,
        in_specs=[anywhere()] * (2 * SIDE),
        out_specs=[vmem()] * 4,
        out_shape=[jax.ShapeDtypeStruct((PANEL, width(part)), jnp.bfloat16) for part in PARTS for _ in range(2)],
        scratch_shapes=[pltpu.SemaphoreType.DMA((4 * SIDE,))],
        name="assemble",
    )(*sum(state, []))


def products_kernel(count, before, after, *refs):
    ins, refs = [refs[4 * n : 4 * n + 4] for n in range(count)], refs[4 * count :]
    if before:
        sum_ref, refs = refs[0], refs[1:]
    outs, refs = (refs[:1], refs[1:]) if after else (refs[:2], refs[2:])
    works, sems = refs[:count], refs[count]
    acc_ref = outs[0] if after else refs[-1]

    def copies(n, p):
        piece = works[n].shape[2] // PIECES
        columns = pl.ds(p * piece, piece)
        return [
            pltpu.make_async_copy(ins[n][i].at[:, columns], works[n].at[i, :, columns], sems.at[n * PIECES + p, i])
            for i in range(4)
        ]

    for n in range(count):
        for p in range(PIECES):
            for copy in copies(n, p):
                copy.start()
    acc_ref[...] = sum_ref[...] if before else jnp.zeros_like(acc_ref)
    for n in range(count):
        piece = works[n].shape[2] // PIECES
        for p in range(PIECES):
            for copy in copies(n, p):
                copy.wait()
            columns = slice(p * piece, (p + 1) * piece)
            left = works[n][:, :, columns].reshape(2 * LEAD, piece)
            lead = works[n][2:, :, columns].reshape(LEAD, piece)
            acc_ref[...] += lax.dot_general(left, lead, TN, preferred_element_type=jnp.float32)
    if not after:
        send_ref, keep_ref = outs
        share = PANEL // 2
        mine = lax.axis_index("col") * share
        other = share - mine
        for c in range(2):
            here = pl.ds(c * share, share)
            keep_ref[here, :] = acc_ref[pl.ds(pl.multiple_of(c * PANEL + mine, share), share), :]
            send_ref[here, :] = acc_ref[pl.ds(pl.multiple_of(c * PANEL + other, share), share), :]
        keep_ref[PANEL:, :] = acc_ref[LEAD:, :]
        send_ref[PANEL:, :] = acc_ref[LEAD:, :]


def add_products(chunks, total, after=True):
    widths = [chunk[0].shape[1] for chunk in chunks]
    acc = (2 * LEAD, LEAD)
    shapes = [acc] if after else [(PANEL + LEAD, LEAD)] * 2
    scratch = [pltpu.VMEM((4, PANEL, columns), jnp.bfloat16) for columns in widths]
    scratch.append(pltpu.SemaphoreType.DMA((len(chunks) * PIECES, 4)))
    if not after:
        scratch.append(pltpu.VMEM(acc, jnp.float32))
    arrays = [array for chunk in chunks for array in chunk]
    sums = [] if total is None else [total]
    return pl.pallas_call(
        functools.partial(products_kernel, len(chunks), total is not None, after),
        in_specs=[anywhere()] * len(arrays) + [vmem()] * len(sums),
        out_specs=[vmem()] * len(shapes),
        out_shape=[jax.ShapeDtypeStruct(shape, jnp.float32) for shape in shapes],
        scratch_shapes=scratch,
        cost_estimate=pl.CostEstimate(
            flops=4 * LEAD * LEAD * sum(widths), bytes_accessed=8 * PANEL * sum(widths), transcendentals=0
        ),
        name="add_products",
    )(*arrays, *sums)


def matern(left, right_x, right_y):
    diff_x = left[:, 0:1] - right_x
    diff_y = left[:, 1:2] - right_y
    t = SQRT_THREE * jnp.sqrt(diff_x * diff_x + diff_y * diff_y) / LENGTH_SCALE
    return (1.0 + t) * jnp.exp(-t)


def eliminate(work_ref, top):
    start = top // PANEL
    lanes = [slice(w * PANEL, (w + 1) * PANEL) for w in range(start, 3)]
    tile = (8, PANEL)
    part = [[work_ref[top + q * 8 : top + q * 8 + 8, w] for w in lanes] for q in range(SUB // 8)]
    for k in range(0, SUB, MINI):
        at = top + k - start * PANEL
        q, sub = k // 8, k % 8
        rows = [[jnp.broadcast_to(t[sub + i : sub + i + 1, :], tile) for t in part[q]] for i in range(MINI)]
        block = [
            [jnp.broadcast_to(rows[i][0][:, at + j : at + j + 1], tile) for j in range(i + 1)] for i in range(MINI)
        ]
        cols = [
            [jnp.broadcast_to(part[p][0][:, at + i : at + i + 1], tile) for p in range(q, SUB // 8)]
            for i in range(MINI)
        ]
        for i in range(MINI):
            inv = lax.rsqrt(block[i][i])
            rows[i] = [t * inv for t in rows[i]]
            cols[i] = [t * inv for t in cols[i]]
            low = {j: block[j][i] * inv for j in range(i + 1, MINI)}
            for j in range(i + 1, MINI):
                for m in range(i + 1, j + 1):
                    block[j][m] = block[j][m] - low[j] * low[m]
                rows[j] = [t - low[j] * u for t, u in zip(rows[j], rows[i])]
                cols[j] = [t - low[j] * u for t, u in zip(cols[j], cols[i])]
            for w, t in zip(lanes, rows[i]):
                work_ref[top + k + i : top + k + i + 1, w] = t[0:1, :]
        for p in range(q, SUB // 8):
            for w in range(len(lanes)):
                change = cols[0][p - q] * rows[0][w]
                for i in range(1, MINI):
                    change = change + cols[i][p - q] * rows[i][w]
                part[p][w] = part[p][w] - change


def finish_kernel(first_ref, jitter_ref, keep_ref, recv_ref, own_ref, leadc_ref, leadr_ref, out_ref, work_ref):
    jitter = jitter_ref[0]
    lead_x, lead_y = leadr_ref[0:1, :], leadr_ref[1:2, :]
    share = PANEL // 2

    def eye(rows, first):
        row = lax.broadcasted_iota(jnp.int32, (rows, LEAD), 0) + first
        col = lax.broadcasted_iota(jnp.int32, (rows, LEAD), 1)
        return jnp.where(row == col, jitter, 0.0)

    block = matern(leadc_ref[...], lead_x, lead_y) + eye(LEAD, 0) - (keep_ref[PANEL:, :] + recv_ref[PANEL:, :])
    work_ref[:, :LEAD] = 0.5 * (block + block.T)
    diag = jnp.concatenate([eye(share, first_ref[0]), eye(share, first_ref[1])], axis=0)
    own = matern(own_ref[...], lead_x, lead_y) + diag - (keep_ref[:PANEL, :] + recv_ref[:PANEL, :])
    work_ref[:, LEAD:] = own.T

    for top in range(0, LEAD, SUB):
        eliminate(work_ref, top)
        low = top + SUB
        if low < LEAD:
            begin = low // PANEL * PANEL
            rows = work_ref[top:low, begin:]
            change = lax.dot_general(
                rows[:, : LEAD - begin], rows, TT, precision=HIGHEST, preferred_element_type=jnp.float32
            )
            work_ref[low:, begin:] -= change[low - begin :, :]
    out_ref[...] = work_ref[:, LEAD:].T


def finish(first, jitter, keep, recv, own, leadc, leadr):
    return pl.pallas_call(
        finish_kernel,
        in_specs=[smem(), smem(), vmem(), vmem(), vmem(), vmem(), vmem()],
        out_specs=vmem(),
        out_shape=jax.ShapeDtypeStruct((PANEL, LEAD), jnp.float32),
        scratch_shapes=[pltpu.VMEM((LEAD, LEAD + PANEL), jnp.float32)],
        name="finish",
    )(first, jitter, keep, recv, own, leadc, leadr)


def hop(value, part, axis, shift, sends=lambda place, order: True, cores=range(2)):
    pairs = []
    for device in range(2 * CHIPS):
        place, order = coordinates(device // 2), ORDERS[part][device % 2]
        if device % 2 in cores and sends(place, order):
            to = {**place, order[axis]: (place[order[axis]] + shift) % SIDE}
            pairs.append((device, 2 * number(to) + device % 2))
    return lax.ppermute(value, ("row", "col"), pairs)


def spread(values, part, axis, sends=lambda place, order: True, cores=range(2)):
    if not isinstance(values, (list, tuple)):
        values = [values] * SIDE
    return [values[0]] + [hop(values[s], part, axis, s, sends, cores) for s in range(1, SIDE)]


def is_root(place):
    return place["x"] < 2 and place["y"] == 0 and place["z"] == 0


def has_chunk(place, order):
    return is_root({**place, order[0]: 0})


def has_piece(place, order):
    return is_root({**place, order[0]: 0, order[1]: 0})


def on_device(factor, scales, coords, jitter):
    row_index, col_index = lax.axis_index("row"), lax.axis_index("col")
    share = PANEL // 2
    begin = row_index * PANEL + col_index * share
    own = lax.dynamic_slice_in_dim(coords, begin, share, 2).reshape(2, PANEL).T
    lead = coords[:, 0, :LEAD]
    lead_t = lead.T
    first = jnp.stack([begin, begin + coords.shape[2]]).astype(jnp.int32)
    barrier = lax.optimization_barrier

    sent, state, after = [None, None], [None, None], factor
    for part in (1, 0):
        sent[part] = dequantize_chunks(part, 0, after, scales)
        state[part] = spread(sent[part], part, 0, lambda place, order: is_root(place))
        after, sent[part] = barrier((factor, sent[part]))
    rest = [dequantize_chunks(part, 1, factor, scales) for part in PARTS]
    state, rest, own, lead, lead_t, first = barrier((state, rest, own, lead, lead_t, first))

    def chunk(part, behind, one, two):
        return sent[part][-behind % SIDE], rest[part][-behind % SIDE], one[part], two[part]

    state = pick_rows(state)
    state = barrier([spread(state[part], part, 1, has_chunk) for part in PARTS])
    zero, one, both = pick_pieces(state)
    zero, both = spread(zero, 0, 2, has_piece), spread(both, 1, 2, has_piece)
    one = spread(one, 0, 2, has_piece, (1,))
    state = pick_shared(*barrier((zero, one, both)))
    state = barrier([spread(state[part], part, 1) for part in PARTS])
    held = assemble(state)
    one, two = held[0::2], held[1::2]
    up_one = [hop(one[part], part, 0, 1) for part in PARTS]
    down_two = [hop(two[part], part, 0, -1) for part in PARTS]
    up_two = [hop(two[part], part, 0, 1) for part in PARTS]
    down_one = [hop(one[part], part, 0, -1) for part in PARTS]
    up_one[1], *kept = barrier((up_one[1], *one, *two))
    (total,) = add_products([chunk(part, 0, kept[:2], kept[2:]) for part in PARTS], None)
    up_one, down_two, up_two, down_one, total = barrier((up_one, down_two, up_two, down_one, total))
    far_one = [hop(up_one[part], part, 0, 1) for part in PARTS]
    far_two = [hop(down_two[part], part, 0, -1) for part in PARTS]
    near = [(1, up_one, up_two), (3, down_one, down_two)]
    (total,) = add_products([chunk(part, *args) for part in PARTS for args in near], total)
    far_one, far_two, total = barrier((far_one, far_two, total))
    send, keep = add_products([chunk(part, 2, far_one, far_two) for part in PARTS], total, after=False)
    recv = lax.ppermute(send, "col", [(0, 1), (1, 0)])
    out = finish(first, jitter, keep, recv, own, lead_t, lead)
    return out.reshape(2, share, LEAD)


def solution(mesh):
    placed = (P(None, "row", "col"), P(None, "row", "col"), P(), P())
    return jax.shard_map(
        on_device,
        mesh=mesh,
        in_specs=placed,
        out_specs=P(None, ("row", "col"), None),
        check_vma=False,
    )
```

```python
import functools

import jax
import jax.numpy as jnp
from jax import lax
from jax.experimental import pallas as pl
from jax.experimental.pallas import tpu as pltpu
from jax.sharding import PartitionSpec as P

PANEL = 128
LEAD = 2 * PANEL
SQRT_THREE = 1.7320508075688772
LENGTH_SCALE = 0.25
HIGHEST = lax.Precision.HIGHEST
TN = (((1,), (1,)), ((), ()))
TT = (((0,), (0,)), ((), ()))

SUB = 64
MINI = 8
QUARTER = PANEL // 4
SIDE = 4
CHIPS = SIDE**3
ORDERS = ((("y", "z", "x"), ("z", "x", "y")), (("x", "y", "z"), ("x", "y", "z")))
BLOCKS = (176, 80)
SLOTS = (1, 2)
PARTS = range(2)
PIECES = 2


def vmem():
    return pl.BlockSpec(memory_space=pltpu.VMEM)


def smem():
    return pl.BlockSpec(memory_space=pltpu.SMEM)


def anywhere():
    return pl.BlockSpec(memory_space=pltpu.HBM)


def width(part):
    return BLOCKS[part] // SIDE * PANEL


def either():
    return pl.BlockSpec(memory_space=pl.ANY)


SMALL = pltpu.CompilerParams(vmem_limit_bytes=12 * 2**20)


def coordinates(chip):
    return {"x": chip % SIDE, "y": chip // SIDE % SIDE, "z": chip // (SIDE * SIDE)}


def number(place):
    return place["x"] + SIDE * place["y"] + SIDE * SIDE * place["z"]


def here(part, axis, root=0):
    place = coordinates(lax.axis_index("row"))
    first, second = [place[order[axis]] - (root if order[axis] == "x" else 0) for order in ORDERS[part]]
    distance = first if ORDERS[part][0] == ORDERS[part][1] else jnp.where(lax.axis_index("col") == 0, first, second)
    return lax.rem(distance + SIDE, SIDE)


def first_block(part, behind):
    return sum(BLOCKS[:part]) + lax.rem(here(part, 0) + SIDE - behind, SIDE) * (BLOCKS[part] // SIDE)


def quarter(part, behind):
    q = lax.rem(here(part, 1) + SIDE - behind, SIDE)
    return pl.ds(pl.multiple_of(q * QUARTER, QUARTER), QUARTER)


def scale_in_place(ref, begin, count, scale_ref, row, first):
    for j in range(count):
        columns = slice((begin + j) * PANEL, (begin + j + 1) * PANEL)
        ref[:, columns] = (ref[:, columns].astype(jnp.float32) * scale_ref[row, 0, first + begin + j]).astype(jnp.bfloat16)


def dequant_kernel(part, cycle, scale_ref, factor_ref, *refs):
    outs, work_ref, in_sems, out_sems = refs[:SIDE], refs[SIDE], refs[SIDE + 1], refs[SIDE + 2]
    columns = work_ref.shape[2]

    def fetch(s):
        begin = pl.multiple_of(first_block(part, SIDE - s) * PANEL, PANEL)
        return pltpu.make_async_copy(factor_ref.at[cycle, :, pl.ds(begin, columns)], work_ref.at[s], in_sems.at[s])

    def put(s):
        return pltpu.make_async_copy(work_ref.at[s], outs[s], out_sems.at[s])

    for s in range(SIDE):
        fetch(s).start()
    for s in range(SIDE):
        fetch(s).wait()
        scale_in_place(work_ref.at[s], 0, columns // PANEL, scale_ref, cycle, first_block(part, SIDE - s))
        put(s).start()
    for s in range(SIDE):
        put(s).wait()


def dequantize_chunks(part, cycle, factor, scales):
    shape = (PANEL, width(part))
    return pl.pallas_call(
        functools.partial(dequant_kernel, part, cycle),
        in_specs=[smem(), anywhere()],
        out_specs=[anywhere()] * SIDE,
        out_shape=[jax.ShapeDtypeStruct(shape, jnp.bfloat16)] * SIDE,
        scratch_shapes=[
            pltpu.VMEM((SIDE, *shape), jnp.bfloat16),
            pltpu.SemaphoreType.DMA((SIDE,)),
            pltpu.SemaphoreType.DMA((SIDE,)),
        ],
        name="dequantize_chunks",
    )(scales, factor)


def gather_copies(moves, sems):
    for n, (wanted, sources, target) in enumerate(moves):
        if len(sources) == 1:
            pltpu.make_async_copy(sources[0], target, sems.at[n]).start()
            continue
        for s, source in enumerate(sources):

            @pl.when(wanted == s)
            def _():
                pltpu.make_async_copy(source, target, sems.at[n]).start()

    for n, (_, sources, target) in enumerate(moves):
        pltpu.make_async_copy(sources[0], target, sems.at[n]).wait()


def of_part(refs, part):
    return refs[part * SIDE : (part + 1) * SIDE]


def pick_rows_kernel(*refs):
    ins, outs, sems = refs[: 2 * SIDE], refs[2 * SIDE : -1], refs[-1]
    moves = []
    for part in PARTS:
        for t in range(SIDE):
            for r in range(SLOTS[part]):
                sources = [ref.at[quarter(part, SIDE - t), :] for ref in of_part(ins, part)]
                moves.append((here(part, 0, r), sources, of_part(outs, part)[t].at[r]))
    gather_copies(moves, sems)


def pick_rows(state):
    out = pl.pallas_call(
        pick_rows_kernel,
        in_specs=[either()] * (2 * SIDE),
        out_specs=[vmem()] * (2 * SIDE),
        out_shape=[
            jax.ShapeDtypeStruct((SLOTS[part], QUARTER, width(part)), jnp.bfloat16)
            for part in PARTS
            for _ in range(SIDE)
        ],
        scratch_shapes=[pltpu.SemaphoreType.DMA((SIDE * sum(SLOTS),))],
        compiler_params=SMALL,
        name="pick_rows",
    )(*sum(state, []))
    return [out[:SIDE], out[SIDE:]]


def pick_pieces_kernel(*refs):
    ins, outs, sems = refs[: 2 * SIDE], (refs[2 * SIDE], refs[2 * SIDE + 1], refs[2 * SIDE + 2]), refs[-1]
    targets = [[outs[0].at[0], outs[1].at[0]], [outs[2].at[0], outs[2].at[1]]]
    moves = []
    for part in PARTS:
        for r in range(2):
            sources = [ref.at[min(r, SLOTS[part] - 1)] for ref in of_part(ins, part)]
            moves.append((here(part, 1, r), sources, targets[part][r]))
    gather_copies(moves, sems)


def pick_pieces(state):
    return pl.pallas_call(
        pick_pieces_kernel,
        in_specs=[either()] * (2 * SIDE),
        out_specs=[vmem()] * 3,
        out_shape=[
            jax.ShapeDtypeStruct((slots, QUARTER, width(part)), jnp.bfloat16) for part, slots in ((0, 1), (0, 1), (1, 2))
        ],
        scratch_shapes=[pltpu.SemaphoreType.DMA((4,))],
        compiler_params=SMALL,
        name="pick_pieces",
    )(*sum(state, []))


def pick_shared_kernel(*refs):
    zero, one, both, outs, sems = refs[:4], refs[4:8], refs[8:12], refs[12:14], refs[-1]
    second = lax.axis_index("col") == 1
    moves = [(here(0, 2, 0), [ref.at[0] for ref in zero], outs[0].at[0])]
    wanted = here(0, 2, 1) + jnp.where(second, SIDE, 0)
    moves.append((wanted, [ref.at[0] for ref in zero] + [ref.at[0] for ref in one], outs[0].at[1]))
    moves += [(here(1, 2, r), [ref.at[r] for ref in both], outs[1].at[r]) for r in range(2)]
    gather_copies(moves, sems)


def pick_shared(zero, one, both):
    return pl.pallas_call(
        pick_shared_kernel,
        in_specs=[either()] * (3 * SIDE),
        out_specs=[vmem()] * 2,
        out_shape=[jax.ShapeDtypeStruct((2, QUARTER, width(part)), jnp.bfloat16) for part in PARTS],
        scratch_shapes=[pltpu.SemaphoreType.DMA((4,))],
        compiler_params=SMALL,
        name="pick_shared",
    )(*zero, *one, *both)


def assemble_kernel(*refs):
    ins, outs, sems = refs[: 2 * SIDE], refs[2 * SIDE : -1], refs[-1]
    moves = []
    for part in PARTS:
        for t in range(SIDE):
            for r in range(2):
                moves.append((0, [of_part(ins, part)[t].at[r]], outs[2 * part + r].at[quarter(part, t), :]))
    gather_copies(moves, sems)


def assemble(state):
    return pl.pallas_call(
        assemble_kernel,
        in_specs=[either()] * (2 * SIDE),
        out_specs=[vmem()] * 4,
        out_shape=[jax.ShapeDtypeStruct((PANEL, width(part)), jnp.bfloat16) for part in PARTS for _ in range(2)],
        scratch_shapes=[pltpu.SemaphoreType.DMA((4 * SIDE,))],
        compiler_params=SMALL,
        name="assemble",
    )(*sum(state, []))


def products_kernel(count, before, after, *refs):
    ins, refs = [refs[4 * n : 4 * n + 4] for n in range(count)], refs[4 * count :]
    if before:
        sum_ref, refs = refs[0], refs[1:]
    outs, refs = (refs[:1], refs[1:]) if after else (refs[:2], refs[2:])
    works, sems = refs[:count], refs[count]
    acc_ref = outs[0] if after else refs[-1]

    def copies(n, p):
        piece = works[n].shape[2] // PIECES
        columns = pl.ds(p * piece, piece)
        return [
            pltpu.make_async_copy(ins[n][i].at[:, columns], works[n].at[i, :, columns], sems.at[n * PIECES + p, i])
            for i in range(4)
        ]

    for n in range(count):
        for p in range(PIECES):
            for copy in copies(n, p):
                copy.start()
    acc_ref[...] = sum_ref[...] if before else jnp.zeros_like(acc_ref)
    for n in range(count):
        piece = works[n].shape[2] // PIECES
        for p in range(PIECES):
            for copy in copies(n, p):
                copy.wait()
            columns = slice(p * piece, (p + 1) * piece)
            left = works[n][:, :, columns].reshape(2 * LEAD, piece)
            lead = works[n][2:, :, columns].reshape(LEAD, piece)
            acc_ref[...] += lax.dot_general(left, lead, TN, preferred_element_type=jnp.float32)
    if not after:
        send_ref, keep_ref = outs
        share = PANEL // 2
        mine = lax.axis_index("col") * share
        other = share - mine
        for c in range(2):
            here = pl.ds(c * share, share)
            keep_ref[here, :] = acc_ref[pl.ds(pl.multiple_of(c * PANEL + mine, share), share), :]
            send_ref[here, :] = acc_ref[pl.ds(pl.multiple_of(c * PANEL + other, share), share), :]
        keep_ref[PANEL:, :] = acc_ref[LEAD:, :]
        send_ref[PANEL:, :] = acc_ref[LEAD:, :]


def add_products(chunks, total, after=True):
    widths = [chunk[0].shape[1] for chunk in chunks]
    acc = (2 * LEAD, LEAD)
    shapes = [acc] if after else [(PANEL + LEAD, LEAD)] * 2
    scratch = [pltpu.VMEM((4, PANEL, columns), jnp.bfloat16) for columns in widths]
    scratch.append(pltpu.SemaphoreType.DMA((len(chunks) * PIECES, 4)))
    if not after:
        scratch.append(pltpu.VMEM(acc, jnp.float32))
    arrays = [array for chunk in chunks for array in chunk]
    sums = [] if total is None else [total]
    return pl.pallas_call(
        functools.partial(products_kernel, len(chunks), total is not None, after),
        in_specs=[either()] * len(arrays) + [vmem()] * len(sums),
        out_specs=[vmem()] * len(shapes),
        out_shape=[jax.ShapeDtypeStruct(shape, jnp.float32) for shape in shapes],
        scratch_shapes=scratch,
        cost_estimate=pl.CostEstimate(
            flops=4 * LEAD * LEAD * sum(widths), bytes_accessed=8 * PANEL * sum(widths), transcendentals=0
        ),
        compiler_params=pltpu.CompilerParams(vmem_limit_bytes=8 * PANEL * sum(widths) + 6 * 2**20),
        name="add_products",
    )(*arrays, *sums)


def matern(left, right_x, right_y):
    diff_x = left[:, 0:1] - right_x
    diff_y = left[:, 1:2] - right_y
    t = SQRT_THREE * jnp.sqrt(diff_x * diff_x + diff_y * diff_y) / LENGTH_SCALE
    return (1.0 + t) * jnp.exp(-t)


def eliminate(work_ref, top):
    start = top // PANEL
    lanes = [slice(w * PANEL, (w + 1) * PANEL) for w in range(start, 3)]
    tile = (8, PANEL)
    part = [[work_ref[top + q * 8 : top + q * 8 + 8, w] for w in lanes] for q in range(SUB // 8)]
    for k in range(0, SUB, MINI):
        at = top + k - start * PANEL
        q, sub = k // 8, k % 8
        rows = [[jnp.broadcast_to(t[sub + i : sub + i + 1, :], tile) for t in part[q]] for i in range(MINI)]
        block = [
            [jnp.broadcast_to(rows[i][0][:, at + j : at + j + 1], tile) for j in range(i + 1)] for i in range(MINI)
        ]
        cols = [
            [jnp.broadcast_to(part[p][0][:, at + i : at + i + 1], tile) for p in range(q, SUB // 8)]
            for i in range(MINI)
        ]
        for i in range(MINI):
            inv = lax.rsqrt(block[i][i])
            rows[i] = [t * inv for t in rows[i]]
            cols[i] = [t * inv for t in cols[i]]
            low = {j: block[j][i] * inv for j in range(i + 1, MINI)}
            for j in range(i + 1, MINI):
                for m in range(i + 1, j + 1):
                    block[j][m] = block[j][m] - low[j] * low[m]
                rows[j] = [t - low[j] * u for t, u in zip(rows[j], rows[i])]
                cols[j] = [t - low[j] * u for t, u in zip(cols[j], cols[i])]
            for w, t in zip(lanes, rows[i]):
                work_ref[top + k + i : top + k + i + 1, w] = t[0:1, :]
        for p in range(q, SUB // 8):
            for w in range(len(lanes)):
                change = cols[0][p - q] * rows[0][w]
                for i in range(1, MINI):
                    change = change + cols[i][p - q] * rows[i][w]
                part[p][w] = part[p][w] - change


def covariance_kernel(first_ref, jitter_ref, own_ref, leadc_ref, leadr_ref, out_ref):
    jitter = jitter_ref[0]
    lead_x, lead_y = leadr_ref[0:1, :], leadr_ref[1:2, :]
    share = PANEL // 2

    def eye(rows, first):
        row = lax.broadcasted_iota(jnp.int32, (rows, LEAD), 0) + first
        col = lax.broadcasted_iota(jnp.int32, (rows, LEAD), 1)
        return jnp.where(row == col, jitter, 0.0)

    diag = jnp.concatenate([eye(share, first_ref[0]), eye(share, first_ref[1])], axis=0)
    out_ref[:PANEL, :] = matern(own_ref[...], lead_x, lead_y) + diag
    out_ref[PANEL:, :] = matern(leadc_ref[...], lead_x, lead_y) + eye(LEAD, 0)


def covariance(first, jitter, own, leadc, leadr):
    return pl.pallas_call(
        covariance_kernel,
        in_specs=[smem(), smem(), vmem(), vmem(), vmem()],
        out_specs=vmem(),
        out_shape=jax.ShapeDtypeStruct((PANEL + LEAD, LEAD), jnp.float32),
        name="covariance",
    )(first, jitter, own, leadc, leadr)


def finish_kernel(cov_ref, keep_ref, recv_ref, out_ref, work_ref):
    block = cov_ref[PANEL:, :] - (keep_ref[PANEL:, :] + recv_ref[PANEL:, :])
    work_ref[:, :LEAD] = 0.5 * (block + block.T)
    work_ref[:, LEAD:] = (cov_ref[:PANEL, :] - (keep_ref[:PANEL, :] + recv_ref[:PANEL, :])).T
    for top in range(0, LEAD, SUB):
        eliminate(work_ref, top)
        low = top + SUB
        if low < LEAD:
            begin = low // PANEL * PANEL
            rows = work_ref[top:low, begin:]
            change = lax.dot_general(
                rows[:, : LEAD - begin], rows, TT, precision=HIGHEST, preferred_element_type=jnp.float32
            )
            work_ref[low:, begin:] -= change[low - begin :, :]
    out_ref[...] = work_ref[:, LEAD:].T


def finish(cov, keep, recv):
    return pl.pallas_call(
        finish_kernel,
        in_specs=[vmem(), vmem(), vmem()],
        out_specs=vmem(),
        out_shape=jax.ShapeDtypeStruct((PANEL, LEAD), jnp.float32),
        scratch_shapes=[pltpu.VMEM((LEAD, LEAD + PANEL), jnp.float32)],
        name="finish",
    )(cov, keep, recv)


def hop(value, part, axis, shift, sends=lambda place, order: True, cores=range(2)):
    pairs = []
    for device in range(2 * CHIPS):
        place, order = coordinates(device // 2), ORDERS[part][device % 2]
        if device % 2 in cores and sends(place, order):
            to = {**place, order[axis]: (place[order[axis]] + shift) % SIDE}
            pairs.append((device, 2 * number(to) + device % 2))
    return lax.ppermute(value, ("row", "col"), pairs)


def spread(values, part, axis, sends=lambda place, order: True, cores=range(2)):
    if not isinstance(values, (list, tuple)):
        values = [values] * SIDE
    return [values[0]] + [hop(values[s], part, axis, s, sends, cores) for s in range(1, SIDE)]


def is_root(place):
    return place["x"] < 2 and place["y"] == 0 and place["z"] == 0


def has_chunk(place, order):
    return is_root({**place, order[0]: 0})


def has_piece(place, order):
    return is_root({**place, order[0]: 0, order[1]: 0})


def on_device(factor, scales, coords, jitter):
    row_index, col_index = lax.axis_index("row"), lax.axis_index("col")
    share = PANEL // 2
    begin = row_index * PANEL + col_index * share
    own = lax.dynamic_slice_in_dim(coords, begin, share, 2).reshape(2, PANEL).T
    lead = coords[:, 0, :LEAD]
    lead_t = lead.T
    first = jnp.stack([begin, begin + coords.shape[2]]).astype(jnp.int32)
    barrier = lax.optimization_barrier

    sent, state, after = [None, None], [None, None], factor
    for part in (1, 0):
        sent[part] = dequantize_chunks(part, 0, after, scales)
        state[part] = spread(sent[part], part, 0, lambda place, order: is_root(place))
        after, sent[part] = barrier((factor, sent[part]))
    rest = [dequantize_chunks(part, 1, factor, scales) for part in PARTS]
    cov = covariance(first, jitter, own, lead_t, lead)
    state, rest, cov = barrier((state, rest, cov))

    def chunk(part, behind, one, two):
        return sent[part][-behind % SIDE], rest[part][-behind % SIDE], one[part], two[part]

    state = pick_rows(state)
    state = barrier([spread(state[part], part, 1, has_chunk) for part in PARTS])
    zero, one, both = pick_pieces(state)
    zero, both = spread(zero, 0, 2, has_piece), spread(both, 1, 2, has_piece)
    one = spread(one, 0, 2, has_piece, (1,))
    state = pick_shared(*barrier((zero, one, both)))
    state = barrier([spread(state[part], part, 1) for part in PARTS])
    held = assemble(state)
    one, two = held[0::2], held[1::2]
    up_one = [hop(one[part], part, 0, 1) for part in PARTS]
    down_two = [hop(two[part], part, 0, -1) for part in PARTS]
    up_two = [hop(two[part], part, 0, 1) for part in PARTS]
    down_one = [hop(one[part], part, 0, -1) for part in PARTS]
    up_one[1], *kept = barrier((up_one[1], *one, *two))
    (total,) = add_products([chunk(part, 0, kept[:2], kept[2:]) for part in PARTS], None)
    up_one, down_two, up_two, down_one, total = barrier((up_one, down_two, up_two, down_one, total))
    far_one = [hop(up_one[part], part, 0, 1) for part in PARTS]
    far_two = [hop(down_two[part], part, 0, -1) for part in PARTS]
    near = [(1, up_one, up_two), (3, down_one, down_two)]
    (total,) = add_products([chunk(part, *args) for part in PARTS for args in near], total)
    far_one, far_two, total = barrier((far_one, far_two, total))
    send, keep = add_products([chunk(part, 2, far_one, far_two) for part in PARTS], total, after=False)
    recv = lax.ppermute(send, "col", [(0, 1), (1, 0)])
    out = finish(cov, keep, recv)
    return out.reshape(2, share, LEAD)


def solution(mesh):
    placed = (P(None, "row", "col"), P(None, "row", "col"), P(), P())
    return jax.shard_map(
        on_device,
        mesh=mesh,
        in_specs=placed,
        out_specs=P(None, ("row", "col"), None),
        check_vma=False,
    )
```
